32 devices in a mesh: aux: 8 (over z, x), grp: 4 (over y, core).
Axes of the slice: x: 2, y: 2, z: 4, core: 2. Of those that a mesh axis runs over, the one named last changes fastest.
Arguments:
- source: float32 [1024, 256], P(('aux', 'grp')), may hold values from -6 to 6
- vir_energy: float32 [1024], P(('aux', 'grp')), may hold values from 0.5 to 3
- occ_energy: float32 [256], replicated, may hold values from -2 to -0.5
- factor_vv: float32 [64, 1024, 1024], P(('aux', 'grp')), may hold values from -0.375 to 0.375
- factor_oo: float32 [64, 256, 256], P(('aux', 'grp')), may hold values from -0.046875 to 0.046875
Outputs:
- response: float32 [1024, 256], P(('aux', 'grp'))
The draws below stay inside these ranges and needn't reach their ends.
All inputs are finite; a program needn't handle non-finite values.
Results may differ from the reference program's by a relative error of at most 0.0001.
Values sent between devices are 32-bit elements; how exact they have to be, the bound alone decides.
A program may use at most 64 MiB of HBM per device.

```python
import jax
import jax.numpy as jnp
from jax import lax

NV = 1024
NO = 256
ITERS = 2
NAUX = 64


def with_spikes(entries, stream_key, source, target, parts, factor):
    owner, partner = [(jnp.arange(entries.shape[position]) // (entries.shape[position] // parts)).reshape([-1 if axis == position else 1 for axis in range(entries.ndim)]) for position in (source, target)]
    chosen = jax.random.permutation(stream_key, parts)[partner]
    strong = (owner == chosen) | (owner == (partner + parts // 2) % parts)
    return jnp.where(strong, factor * entries, entries)


def steps_of(own_key, extent, shards, smallest, largest):
    factor_of = 1.0
    for axis_at, parts in shards:
        draws = jax.random.uniform(jax.random.fold_in(jax.random.fold_in(own_key, 6), axis_at), (parts,), jnp.float32, smallest / len(shards), largest / len(shards))
        factor_of = factor_of * jnp.repeat(jnp.exp(draws), extent[axis_at] // parts).reshape((-1,) + (1,) * (len(extent) - 1 - axis_at))
    return factor_of


def centred(key, shape, spread, most, pieces=(), dtype=jnp.bfloat16):
    factor_of = steps_of(key, shape, pieces, -0.22, 0.18) if pieces else 1.0
    array = jax.random.normal(key, shape, jnp.float32) * spread * factor_of
    return jnp.minimum(jnp.maximum(array, -most), most).astype(dtype)


def noise_with(rng, extent, width, bound, split, heavy, dtype=jnp.bfloat16):
    array = width * jax.random.normal(rng, extent, jnp.float32)
    if split:
        array = array * steps_of(rng, extent, split, -0.22, 0.18)
    return jnp.clip(with_spikes(array, jax.random.fold_in(rng, 3), *heavy), -bound, bound).astype(dtype)


def setup_inputs(seed: int = 0) -> dict:
    seeds = jax.random.split(jax.random.key(seed), 6)
    source = centred(seeds[0], (NV, NO), 1.0, 6.0, ((0, 32),), jnp.float32)
    vir_energy = jnp.clip(0.5 + 2.5 * jax.random.uniform(seeds[1], (NV,), jnp.float32) ** steps_of(seeds[1], (NV,), ((0, 32),), -0.2, 0.2), 0.5, 3.0)
    occ_energy = jnp.clip(jax.random.uniform(seeds[2], (NO,), jnp.float32, -2.0, -0.5), -2.0, -0.5)
    factor_vv = noise_with(seeds[3], (NAUX, NV, NV), NV ** -0.5, 0.375, ((0, 32),), (0, 1, 32, 2.75), jnp.float32)
    factor_oo = centred(seeds[4], (NAUX, NO, NO), (NO * NAUX) ** -0.5, 0.046875, ((0, 32),), jnp.float32)
    return {"source": source, "vir_energy": vir_energy, "occ_energy": occ_energy, "factor_vv": factor_vv, "factor_oo": factor_oo}


def apply_factors(amplitudes, factor_vv, factor_oo):
    def step(total, pair):
        left, right = pair
        inner = jnp.dot(left, amplitudes, precision=lax.Precision.HIGHEST, preferred_element_type=jnp.float32)
        return total + jnp.dot(inner, right, precision=lax.Precision.HIGHEST, preferred_element_type=jnp.float32), None

    start = jnp.zeros(amplitudes.shape, jnp.float32)
    total, _ = lax.scan(step, start, (factor_vv, factor_oo))
    return total


def reference(source, vir_energy, occ_energy, factor_vv, factor_oo):
    gap = vir_energy[:, None] - occ_energy[None, :]
    amplitudes = source / gap
    for sweep in range(ITERS):
        summed = apply_factors(amplitudes, factor_vv, factor_oo)
        amplitudes = (source - summed) / gap
    return amplitudes
```

```python
import functools

import jax
import jax.numpy as jnp
from jax import lax
from jax.experimental import pallas as pl
from jax.experimental.pallas import tpu as pltpu
from jax.sharding import PartitionSpec as P

ITERS = 2
AXES = ("aux", "grp")
F32 = jnp.float32
BF16 = jnp.bfloat16
MESH = pl.DeviceIdType.MESH
GROUPS = 4
HALVES = 2


def split(value):
    high = value.astype(BF16)
    return high, (value - high.astype(F32)).astype(BF16)


def dot3(a, b):
    (ah, al), (bh, bl) = a, b
    dot = functools.partial(jnp.dot, preferred_element_type=F32)
    return dot(ah, bh) + (dot(ah, bl) + dot(al, bh))


def kernel(
    sizes, source, vir, occ, oo, vv, out,
    stage, vh, vl, oh, ol, th, tl, acc, gathered, from_partner, received,
    load_sem, gather_send, gather_recv, pair_send, pair_recv, scatter_send, scatter_recv,
):
    naux, ngrp, rows = sizes
    chips, pairs = naux * ngrp // 2, ngrp // 2
    terms, width = oo.shape[0], oo.shape[1]
    per_group = chips // GROUPS
    span = 2 * per_group * rows
    per_half = chips // HALVES
    tall = per_half * rows
    aux, grp = lax.axis_index("aux"), lax.axis_index("grp")
    core = grp % 2
    chip = aux * pairs + grp // 2

    def device(which, side):
        return (which // pairs, (which % pairs) * 2 + side)

    partner = device(chip, 1 - core)

    loads = []
    for slot in range(2):
        side = (1 - core) if slot == 0 else core
        for p in range(terms):
            load = pltpu.make_async_copy(vv.at[p, :, side], stage.at[slot, p], load_sem.at[slot, p])
            load.start()
            loads.append(load)

    barrier = pltpu.get_barrier_semaphore()
    pl.semaphore_signal(barrier, inc=1, device_id=partner, device_id_type=MESH)
    for o in range(1, chips):
        pl.semaphore_signal(
            barrier, inc=1, device_id=device((chip + o) % chips, core), device_id_type=MESH
        )

    at_row = lax.broadcasted_iota(jnp.int32, (rows, rows), 0)
    at_column = lax.broadcasted_iota(jnp.int32, (rows, rows), 1)
    spread = jnp.broadcast_to(vir[...], (rows, rows))
    vir_column = jnp.sum(jnp.where(at_row == at_column, spread, 0.0), axis=1, keepdims=True)
    gap = vir_column - occ[...]
    mine = source[...] / gap
    own = 2 * chip + core
    gathered[0, own] = mine
    for p in range(terms):
        oh[p], ol[p] = split(oo[p])
    pl.semaphore_wait(barrier, chips)

    home = chip // per_group
    inside = chip % per_group
    order = [(home + g) % GROUPS for g in (0, 1, 3, 2)]

    def peers(g):
        start = order[g] * per_group
        return [start + (inside + o) % per_group for o in range(1 if g == 0 else 0, per_group)]

    def gather_to_partner(it, block):
        return pltpu.make_async_remote_copy(
            gathered.at[it, block], gathered.at[it, block],
            gather_send.at[it, 1, block // 2], gather_recv.at[it, block],
            device_id=partner, device_id_type=MESH,
        )

    def gather_to(it, other):
        return pltpu.make_async_remote_copy(
            gathered.at[it, own], gathered.at[it, own],
            gather_send.at[it, 0, other], gather_recv.at[it, own],
            device_id=device(other, core), device_id_type=MESH,
        )

    def arrival(it, block):
        return pltpu.make_async_remote_copy(
            gathered.at[it, block], gathered.at[it, block],
            gather_send.at[it, 1, block // 2], gather_recv.at[it, block],
            device_id=partner, device_id_type=MESH,
        )

    def start_gather(it):
        sends = []
        for g in (1, 2, 0, 3):
            for other in peers(g):
                sends.append(gather_to(it, other))
                sends[-1].start()
        sends.append(gather_to_partner(it, own))
        sends[-1].start()
        return sends

    def product(q, slot, at):
        place = pl.ds(pl.multiple_of(at * tall, tall), tall)
        total = None
        for p in range(terms):
            term = dot3(
                (vh[q, p, slot, place, :], vl[q, p, slot, place, :]), (th[p], tl[p])
            )
            total = term if total is None else total + term
        return total

    def halfway(it, q):
        piece = gathered[it, pl.ds(q * 2 * per_group, 2 * per_group)].reshape(span, width)
        piece = split(piece)
        for p in range(terms):
            th[p], tl[p] = split(dot3(piece, (oh[p], ol[p])))

    sends = start_gather(0)

    for slot in range(2):
        for p in range(terms):
            loads[slot * terms + p].wait()

            def convert(c, carry):
                value = stage[slot, p, c]
                high, low = split(value)
                place = pl.ds(pl.multiple_of(c * rows, rows), rows)
                for q in range(GROUPS):
                    vh[q, p, slot, place, :] = high[:, q * span:(q + 1) * span]
                    vl[q, p, slot, place, :] = low[:, q * span:(q + 1) * span]
                return carry

            lax.fori_loop(0, chips, convert, 0)

    near = chip // per_half
    far = (near + 1) % HALVES
    within = chip % per_half

    for it in range(ITERS):
        def consume(g):
            q = order[g]
            for other in ([chip] if g == 0 else []) + peers(g):
                arrival(it, 2 * other + 1 - core).wait_recv()
            halfway(it, q)
            return q

        def accumulate(g):
            q = consume(g)

            def step(i, carry):
                slot, at = i // HALVES, i % HALVES
                place = pl.ds(pl.multiple_of(at * tall, tall), tall)
                term = product(q, slot, at)
                if g == 0:
                    acc[slot, place, :] = term
                else:
                    acc[slot, place, :] += term
                return carry

            lax.fori_loop(0, 2 * HALVES, step, 0)

        for g in range(GROUPS):
            for other in peers(g):
                arrival(it, 2 * other + core).wait_recv()
                sends.append(gather_to_partner(it, 2 * other + core))
                sends[-1].start()
            if g > 0:
                accumulate(g - 1)

        q = consume(GROUPS - 1)
        handed = []
        for at in (far, near):
            place = pl.ds(pl.multiple_of(at * tall, tall), tall)
            acc[0, place, :] += product(q, 0, at)
            handed.append(pltpu.make_async_remote_copy(
                acc.at[0, place], from_partner.at[it, at],
                pair_send.at[it, at], pair_recv.at[it, at],
                device_id=partner, device_id_type=MESH,
            ))
            handed[-1].start()

        def scatter_to(other, sender):
            return pltpu.make_async_remote_copy(
                acc.at[1, pl.ds(pl.multiple_of(other * rows, rows), rows)],
                received.at[it, sender],
                scatter_send.at[it, other], scatter_recv.at[it, sender],
                device_id=device(other, core), device_id_type=MESH,
            )

        scattered = []
        others = []
        for n, at in enumerate((far, near)):
            place = pl.ds(pl.multiple_of(at * tall, tall), tall)
            term = product(q, 1, at)
            handed[n].wait_recv()
            acc[1, place, :] += term + from_partner[it, at]
            for o in range(n, per_half):
                other = at * per_half + (within + o) % per_half
                others.append(other)
                scattered.append(scatter_to(other, chip))
                scattered[-1].start()
        summed = acc[1, pl.ds(pl.multiple_of(chip * rows, rows), rows), :]
        for other in others[per_half:] + others[:per_half]:
            scatter_to(other, other).wait_recv()
            summed = summed + received[it, other]
        mine = (source[...] - summed) / gap
        if it + 1 < ITERS:
            gathered[it + 1, own] = mine
            later = start_gather(it + 1)
        else:
            out[...] = mine
            later = []
        for copy in sends + handed + scattered:
            copy.wait_send()
        sends = later


def fused(sizes, source, vir_energy, occ_energy, factor_vv, factor_oo):
    naux, ngrp = sizes
    rows, width = source.shape
    terms, whole, _ = factor_vv.shape
    chips = naux * ngrp // 2
    span = whole // GROUPS
    tall = chips // HALVES * rows
    vmem = pl.BlockSpec(memory_space=pltpu.VMEM)
    dma = pltpu.SemaphoreType.DMA
    return pl.pallas_call(
        functools.partial(kernel, (naux, ngrp, rows)),
        out_shape=jax.ShapeDtypeStruct((rows, width), F32),
        in_specs=[vmem] * 4 + [pl.BlockSpec(memory_space=pl.ANY)],
        out_specs=vmem,
        scratch_shapes=[
            pltpu.VMEM((2, terms, chips, rows, whole), F32),
            pltpu.VMEM((GROUPS, terms, 2, chips * rows, span), BF16),
            pltpu.VMEM((GROUPS, terms, 2, chips * rows, span), BF16),
            pltpu.VMEM((terms, width, width), BF16),
            pltpu.VMEM((terms, width, width), BF16),
            pltpu.VMEM((terms, span, width), BF16),
            pltpu.VMEM((terms, span, width), BF16),
            pltpu.VMEM((2, chips * rows, width), F32),
            pltpu.VMEM((ITERS, 2 * chips, rows, width), F32),
            pltpu.VMEM((ITERS, HALVES, tall, width), F32),
            pltpu.VMEM((ITERS, chips, rows, width), F32),
            dma((2, terms)),
            dma((ITERS, 2, chips)),
            dma((ITERS, 2 * chips)),
            dma((ITERS, HALVES)),
            dma((ITERS, HALVES)),
            dma((ITERS, chips)),
            dma((ITERS, chips)),
        ],
        compiler_params=pltpu.CompilerParams(collective_id=0, has_side_effects=True),
    )(
        source,
        vir_energy.reshape(1, rows),
        occ_energy.reshape(1, width),
        factor_oo,
        factor_vv.reshape(terms, chips, 2, rows, whole),
    )


def plain(source, vir_energy, occ_energy, factor_vv, factor_oo):
    gap = vir_energy[:, None] - occ_energy[None, :]
    einsum = functools.partial(
        jnp.einsum, precision=lax.Precision.HIGHEST, preferred_element_type=F32
    )
    mine = source / gap
    for _ in range(ITERS):
        whole = lax.all_gather(mine, AXES, axis=0, tiled=True)
        terms = einsum("pab,pbj->aj", factor_vv, einsum("bi,pij->pbj", whole, factor_oo))
        summed = lax.psum_scatter(terms, AXES, scatter_dimension=0, tiled=True)
        mine = (source - summed) / gap
    return mine


def local(sizes, source, *rest):
    chips = sizes[0] * sizes[1] // 2
    rows, width = source.shape
    whole = chips * 2 * rows
    fits = (
        rows % 16 == 0 and sizes[1] % 2 == 0 and GROUPS == 4 and chips % GROUPS == 0
        and HALVES == 2 and whole % (GROUPS * 128) == 0 and width % 128 == 0
    )
    return fused(sizes, source, *rest) if fits else plain(source, *rest)


def solution(mesh):
    sizes = (mesh.shape["aux"], mesh.shape["grp"])
    placed = (P(AXES, None), P(AXES), P(), P(AXES, None, None), P(AXES, None, None))
    return jax.shard_map(
        functools.partial(local, sizes),
        mesh=mesh, in_specs=placed, out_specs=P(AXES, None), check_vma=False,
    )
```

```python
import functools

import jax
import jax.numpy as jnp
from jax import lax
from jax.experimental import pallas as pl
from jax.experimental.pallas import tpu as pltpu
from jax.sharding import PartitionSpec as P

ITERS = 2
AXES = ("aux", "grp")
F32 = jnp.float32
BF16 = jnp.bfloat16
MESH = pl.DeviceIdType.MESH
GROUPS = 4
HALVES = 2


def split(value):
    high = value.astype(BF16)
    return high, (value - high.astype(F32)).astype(BF16)


def dot3(a, b):
    (ah, al), (bh, bl) = a, b
    dot = functools.partial(jnp.dot, preferred_element_type=F32)
    return dot(ah, bh) + (dot(ah, bl) + dot(al, bh))


def kernel(
    sizes, source, vir, occ, oo, vv, out,
    stage, vh, vl, oh, ol, th, tl, acc, gathered, from_partner, received,
    load_sem, gather_send, gather_recv, pair_send, pair_recv, scatter_send, scatter_recv,
):
    naux, ngrp, rows = sizes
    chips, pairs = naux * ngrp // 2, ngrp // 2
    terms, width = oo.shape[0], oo.shape[1]
    per_group = chips // GROUPS
    span = 2 * per_group * rows
    per_half = chips // HALVES
    tall = per_half * rows
    aux, grp = lax.axis_index("aux"), lax.axis_index("grp")
    core = grp % 2
    chip = aux * pairs + grp // 2

    def device(which, side):
        return (which // pairs, (which % pairs) * 2 + side)

    z, x, y = aux // 2, aux % 2, grp // 2

    def column(dx, dy):
        return ((x + dx) % 2) * 2 + (y + dy) % 2

    self_, first, second, both = column(0, 0), column(1 - core, core), column(core, 1 - core), column(1, 1)

    def at(plane, col):
        return plane * 4 + col

    partner = device(chip, 1 - core)
    to_first, to_second = device(at(z, first), core), device(at(z, second), core)

    loads = []
    for slot in range(2):
        side = (1 - core) if slot == 0 else core
        for p in range(terms):
            load = pltpu.make_async_copy(vv.at[p, :, side], stage.at[slot, p], load_sem.at[slot, p])
            load.start()
            loads.append(load)

    barrier = pltpu.get_barrier_semaphore()
    pl.semaphore_signal(barrier, inc=1, device_id=partner, device_id_type=MESH)
    order = [z, z + 1 - 2 * (z % 2), 2 - z // 2, 3 - 3 * (z // 2)]
    greeted = [to_first, to_second] + [device(at(plane, self_), core) for plane in order[1:]]
    for other in greeted:
        pl.semaphore_signal(barrier, inc=1, device_id=other, device_id_type=MESH)

    at_row = lax.broadcasted_iota(jnp.int32, (rows, rows), 0)
    at_column = lax.broadcasted_iota(jnp.int32, (rows, rows), 1)
    spread = jnp.broadcast_to(vir[...], (rows, rows))
    vir_column = jnp.sum(jnp.where(at_row == at_column, spread, 0.0), axis=1, keepdims=True)
    gap = vir_column - occ[...]
    mine = source[...] / gap
    own = 2 * chip + core
    gathered[0, own] = mine
    for p in range(terms):
        oh[p], ol[p] = split(oo[p])
    pl.semaphore_wait(barrier, 1 + len(greeted))

    def remote(src, dst, send, recv, target):
        return pltpu.make_async_remote_copy(
            src, dst, send, recv, device_id=target, device_id_type=MESH
        )

    def block_copy(it, block, kind, index, target):
        piece = gathered.at[it, block]
        return remote(piece, piece, gather_send.at[it, kind, index], gather_recv.at[it, block], target)

    def arrived(it, which, side):
        block_copy(it, 2 * which + side, 0, which, partner).wait_recv()

    def pass_on(it, which, sends, targets):
        for kind, target in targets:
            sends.append(block_copy(it, 2 * which + core, kind, which, target))
            sends[-1].start()

    def start_gather(it):
        sends = []
        for plane in order[1:]:
            there = at(plane, self_)
            sends.append(block_copy(it, own, 3, there, device(there, core)))
            sends[-1].start()
        pass_on(it, chip, sends, ((0, to_first), (1, to_second), (2, partner)))
        return sends

    def product(q, slot, half):
        place = pl.ds(pl.multiple_of(half * tall, tall), tall)
        total = None
        for p in range(terms):
            term = dot3(
                (vh[q, p, slot, place, :], vl[q, p, slot, place, :]), (th[p], tl[p])
            )
            total = term if total is None else total + term
        return total

    def halfway(it, q):
        piece = gathered[it, pl.ds(q * 2 * per_group, 2 * per_group)].reshape(span, width)
        piece = split(piece)
        for p in range(terms):
            th[p], tl[p] = split(dot3(piece, (oh[p], ol[p])))

    sends = start_gather(0)

    for slot in range(2):
        for p in range(terms):
            loads[slot * terms + p].wait()

            def convert(c, carry):
                value = stage[slot, p, c]
                high, low = split(value)
                place = pl.ds(pl.multiple_of(c * rows, rows), rows)
                for q in range(GROUPS):
                    vh[q, p, slot, place, :] = high[:, q * span:(q + 1) * span]
                    vl[q, p, slot, place, :] = low[:, q * span:(q + 1) * span]
                return carry

            lax.fori_loop(0, chips, convert, 0)

    near = chip // per_half
    far = (near + 1) % HALVES

    for it in range(ITERS):
        def from_plane(g):
            which = at(order[g], self_)
            arrived(it, which, core)
            pass_on(it, which, sends, ((0, to_first), (1, to_second), (2, partner)))

        def from_first(g):
            which = at(order[g], first)
            arrived(it, which, core)
            pass_on(it, which, sends, ((1, to_second), (2, partner)))

        def from_second(g):
            for col in (second, both):
                which = at(order[g], col)
                arrived(it, which, core)
                pass_on(it, which, sends, ((2, partner),))

        def consume(g):
            for col in (self_, first, second, both):
                arrived(it, at(order[g], col), 1 - core)
            halfway(it, order[g])
            return order[g]

        def accumulate(g):
            q = consume(g)

            def step(i, carry):
                slot, half = i // HALVES, i % HALVES
                place = pl.ds(pl.multiple_of(half * tall, tall), tall)
                term = product(q, slot, half)
                if g == 0:
                    acc[slot, place, :] = term
                else:
                    acc[slot, place, :] += term
                return carry

            lax.fori_loop(0, 2 * HALVES, step, 0)

        from_plane(1)
        from_first(0)
        from_plane(2)
        from_first(1)
        from_second(0)
        from_plane(3)
        from_first(2)
        accumulate(0)
        from_first(3)
        from_second(1)
        accumulate(1)
        from_second(2)
        accumulate(2)
        from_second(3)
        q = consume(3)

        def piece(which):
            return pl.ds(pl.multiple_of(which * rows, rows), rows)

        def scatter(stage_, plane, col, target):
            which = at(plane, col)
            return remote(
                acc.at[1, piece(which)], received.at[it, stage_, which],
                scatter_send.at[it, stage_, which], scatter_recv.at[it, stage_, which], target,
            )

        def to_plane(plane, sender):
            return remote(
                acc.at[1, piece(at(plane, self_))], received.at[it, 2, sender],
                scatter_send.at[it, 2, plane], scatter_recv.at[it, 2, sender],
                device(at(plane, self_), core),
            )

        def begin(copy):
            sends.append(copy)
            copy.start()

        for half in (far, near):
            place = pl.ds(pl.multiple_of(half * tall, tall), tall)
            acc[0, place, :] += product(q, 0, half)
            handed = remote(
                acc.at[0, place], from_partner.at[it, half],
                pair_send.at[it, half], pair_recv.at[it, half], partner,
            )
            begin(handed)
            term = product(q, 1, half)
            handed.wait_recv()
            acc[1, place, :] += term + from_partner[it, half]
            for g in ((3, 2) if half is far else (1, 0)):
                for col in (both, second):
                    begin(scatter(0, order[g], col, to_second))

        def add(stage_, plane, col):
            which = at(plane, col)
            scatter(stage_, plane, col, partner).wait_recv()
            acc[1, piece(which), :] += received[it, stage_, which]

        for g in (3, 2, 1, 0):
            add(0, order[g], first)
            begin(scatter(1, order[g], first, to_first))
            add(0, order[g], self_)
        for g in (3, 2, 1):
            add(1, order[g], self_)
            begin(to_plane(order[g], z))
        add(1, z, self_)
        summed = acc[1, piece(chip), :]
        for g in (1, 2, 3):
            to_plane(order[g], order[g]).wait_recv()
            summed = summed + received[it, 2, order[g]]
        mine = (source[...] - summed) / gap
        if it + 1 < ITERS:
            gathered[it + 1, own] = mine
            later = start_gather(it + 1)
        else:
            out[...] = mine
            later = []
        for copy in sends:
            copy.wait_send()
        sends = later


def fused(sizes, source, vir_energy, occ_energy, factor_vv, factor_oo):
    naux, ngrp = sizes
    rows, width = source.shape
    terms, whole, _ = factor_vv.shape
    chips = naux * ngrp // 2
    span = whole // GROUPS
    tall = chips // HALVES * rows
    vmem = pl.BlockSpec(memory_space=pltpu.VMEM)
    dma = pltpu.SemaphoreType.DMA
    return pl.pallas_call(
        functools.partial(kernel, (naux, ngrp, rows)),
        out_shape=jax.ShapeDtypeStruct((rows, width), F32),
        in_specs=[vmem] * 4 + [pl.BlockSpec(memory_space=pl.ANY)],
        out_specs=vmem,
        scratch_shapes=[
            pltpu.VMEM((2, terms, chips, rows, whole), F32),
            pltpu.VMEM((GROUPS, terms, 2, chips * rows, span), BF16),
            pltpu.VMEM((GROUPS, terms, 2, chips * rows, span), BF16),
            pltpu.VMEM((terms, width, width), BF16),
            pltpu.VMEM((terms, width, width), BF16),
            pltpu.VMEM((terms, span, width), BF16),
            pltpu.VMEM((terms, span, width), BF16),
            pltpu.VMEM((2, chips * rows, width), F32),
            pltpu.VMEM((ITERS, 2 * chips, rows, width), F32),
            pltpu.VMEM((ITERS, HALVES, tall, width), F32),
            pltpu.VMEM((ITERS, 3, chips, rows, width), F32),
            dma((2, terms)),
            dma((ITERS, 4, chips)),
            dma((ITERS, 2 * chips)),
            dma((ITERS, HALVES)),
            dma((ITERS, HALVES)),
            dma((ITERS, 3, chips)),
            dma((ITERS, 3, chips)),
        ],
        compiler_params=pltpu.CompilerParams(collective_id=0, has_side_effects=True),
    )(
        source,
        vir_energy.reshape(1, rows),
        occ_energy.reshape(1, width),
        factor_oo,
        factor_vv.reshape(terms, chips, 2, rows, whole),
    )


def plain(source, vir_energy, occ_energy, factor_vv, factor_oo):
    gap = vir_energy[:, None] - occ_energy[None, :]
    einsum = functools.partial(
        jnp.einsum, precision=lax.Precision.HIGHEST, preferred_element_type=F32
    )
    mine = source / gap
    for _ in range(ITERS):
        whole = lax.all_gather(mine, AXES, axis=0, tiled=True)
        terms = einsum("pab,pbj->aj", factor_vv, einsum("bi,pij->pbj", whole, factor_oo))
        summed = lax.psum_scatter(terms, AXES, scatter_dimension=0, tiled=True)
        mine = (source - summed) / gap
    return mine


def local(sizes, source, *rest):
    chips = sizes[0] * sizes[1] // 2
    rows, width = source.shape
    whole = chips * 2 * rows
    fits = (
        rows % 16 == 0 and sizes == (2 * GROUPS, 4) and GROUPS == 4 and HALVES == 2
        and whole % (GROUPS * 128) == 0 and width % 128 == 0
    )
    return fused(sizes, source, *rest) if fits else plain(source, *rest)


def solution(mesh):
    sizes = (mesh.shape["aux"], mesh.shape["grp"])
    placed = (P(AXES, None), P(AXES), P(), P(AXES, None, None), P(AXES, None, None))
    return jax.shard_map(
        functools.partial(local, sizes),
        mesh=mesh, in_specs=placed, out_specs=P(AXES, None), check_vma=False,
    )
```

```python
import functools

import jax
import jax.numpy as jnp
from jax import lax
from jax.experimental import pallas as pl
from jax.experimental.pallas import tpu as pltpu
from jax.sharding import PartitionSpec as P

ITERS = 2
AXES = ("aux", "grp")
F32 = jnp.float32
BF16 = jnp.bfloat16
MESH = pl.DeviceIdType.MESH
GROUPS = 4
HALVES = 2


def split(value):
    high = value.astype(BF16)
    return high, (value - high.astype(F32)).astype(BF16)


def dot3(a, b):
    (ah, al), (bh, bl) = a, b
    dot = functools.partial(jnp.dot, preferred_element_type=F32)
    return dot(ah, bh) + (dot(ah, bl) + dot(al, bh))


def kernel(
    sizes, source, vir, occ, oo, vv, out,
    stage, vh, vl, oh, ol, th, tl, acc, gathered, from_partner, received,
    load_sem, gather_send, gather_recv, pair_send, pair_recv, scatter_send, scatter_recv,
):
    naux, ngrp, rows = sizes
    chips, pairs = naux * ngrp // 2, ngrp // 2
    terms, width = oo.shape[0], oo.shape[1]
    per_group = chips // GROUPS
    span = 2 * per_group * rows
    per_half = chips // HALVES
    tall = per_half * rows
    aux, grp = lax.axis_index("aux"), lax.axis_index("grp")
    core = grp % 2
    chip = aux * pairs + grp // 2

    def device(which, side):
        return (which // pairs, (which % pairs) * 2 + side)

    z, x, y = aux // 2, aux % 2, grp // 2

    def column(dx, dy):
        return ((x + dx) % 2) * 2 + (y + dy) % 2

    self_, first, second, both = column(0, 0), column(1 - core, core), column(core, 1 - core), column(1, 1)

    def at(plane, col):
        return plane * 4 + col

    partner = device(chip, 1 - core)
    to_first, to_second, to_both = [device(at(z, col), core) for col in (first, second, both)]

    loads = []
    for slot in range(2):
        side = (1 - core) if slot == 0 else core
        for p in range(terms):
            load = pltpu.make_async_copy(vv.at[p, :, side], stage.at[slot, p], load_sem.at[slot, p])
            load.start()
            loads.append(load)

    barrier = pltpu.get_barrier_semaphore()
    pl.semaphore_signal(barrier, inc=1, device_id=partner, device_id_type=MESH)
    order = [z, z + 1 - 2 * (z % 2), 2 - z // 2, 3 - 3 * (z // 2)]
    greeted = [to_first, to_second, to_both] + [device(at(plane, self_), core) for plane in order[1:]]
    for other in greeted:
        pl.semaphore_signal(barrier, inc=1, device_id=other, device_id_type=MESH)

    at_row = lax.broadcasted_iota(jnp.int32, (rows, rows), 0)
    at_column = lax.broadcasted_iota(jnp.int32, (rows, rows), 1)
    spread = jnp.broadcast_to(vir[...], (rows, rows))
    vir_column = jnp.sum(jnp.where(at_row == at_column, spread, 0.0), axis=1, keepdims=True)
    gap = vir_column - occ[...]
    mine = source[...] / gap
    own = 2 * chip + core
    gathered[0, own] = mine
    for p in range(terms):
        oh[p], ol[p] = split(oo[p])
    pl.semaphore_wait(barrier, 1 + len(greeted))

    def remote(src, dst, send, recv, target):
        return pltpu.make_async_remote_copy(
            src, dst, send, recv, device_id=target, device_id_type=MESH
        )

    def block_copy(it, block, kind, index, target):
        piece = gathered.at[it, block]
        return remote(piece, piece, gather_send.at[it, kind, index], gather_recv.at[it, block], target)

    def arrived(it, which, side):
        block_copy(it, 2 * which + side, 0, which, partner).wait_recv()

    def pass_on(it, which, sends, targets):
        for kind, target in targets:
            sends.append(block_copy(it, 2 * which + core, kind, which, target))
            sends[-1].start()

    everyone = ((4, to_both), (0, to_first), (1, to_second), (2, partner))

    def start_gather(it):
        sends = []
        for plane in order[1:]:
            there = at(plane, self_)
            sends.append(block_copy(it, own, 3, there, device(there, core)))
            sends[-1].start()
        pass_on(it, chip, sends, everyone)
        return sends

    def product(q, slot, half):
        place = pl.ds(pl.multiple_of(half * tall, tall), tall)
        total = None
        for p in range(terms):
            term = dot3(
                (vh[q, p, slot, place, :], vl[q, p, slot, place, :]), (th[p], tl[p])
            )
            total = term if total is None else total + term
        return total

    def halfway(it, q):
        piece = gathered[it, pl.ds(q * 2 * per_group, 2 * per_group)].reshape(span, width)
        piece = split(piece)
        for p in range(terms):
            th[p], tl[p] = split(dot3(piece, (oh[p], ol[p])))

    sends = start_gather(0)

    for slot in range(2):
        for p in range(terms):
            loads[slot * terms + p].wait()

            def convert(c, carry):
                value = stage[slot, p, c]
                high, low = split(value)
                place = pl.ds(pl.multiple_of(c * rows, rows), rows)
                for q in range(GROUPS):
                    vh[q, p, slot, place, :] = high[:, q * span:(q + 1) * span]
                    vl[q, p, slot, place, :] = low[:, q * span:(q + 1) * span]
                return carry

            lax.fori_loop(0, chips, convert, 0)

    near = chip // per_half
    far = (near + 1) % HALVES

    for it in range(ITERS):
        def from_plane(g):
            which = at(order[g], self_)
            arrived(it, which, core)
            pass_on(it, which, sends, everyone)

        def from_near(g):
            for col in (first, second, both):
                which = at(order[g], col)
                arrived(it, which, core)
                pass_on(it, which, sends, ((2, partner),))

        def consume(g):
            for col in (self_, first, second, both):
                arrived(it, at(order[g], col), 1 - core)
            halfway(it, order[g])
            return order[g]

        def accumulate(g):
            q = consume(g)

            def step(i, carry):
                slot, half = i // HALVES, i % HALVES
                place = pl.ds(pl.multiple_of(half * tall, tall), tall)
                term = product(q, slot, half)
                if g == 0:
                    acc[slot, place, :] = term
                else:
                    acc[slot, place, :] += term
                return carry

            lax.fori_loop(0, 2 * HALVES, step, 0)

        from_plane(1)
        from_near(0)
        from_plane(2)
        from_plane(3)
        from_near(1)
        accumulate(0)
        from_near(2)
        accumulate(1)
        from_near(3)
        accumulate(2)
        q = consume(3)

        def piece(which):
            return pl.ds(pl.multiple_of(which * rows, rows), rows)

        def scatter(stage_, plane, col, target):
            which = at(plane, col)
            return remote(
                acc.at[1, piece(which)], received.at[it, stage_, which],
                scatter_send.at[it, stage_, which], scatter_recv.at[it, stage_, which], target,
            )

        def to_plane(plane, sender):
            return remote(
                acc.at[1, piece(at(plane, self_))], received.at[it, 3, sender],
                scatter_send.at[it, 3, plane], scatter_recv.at[it, 3, sender],
                device(at(plane, self_), core),
            )

        def begin(copy):
            sends.append(copy)
            copy.start()

        for half in (far, near):
            place = pl.ds(pl.multiple_of(half * tall, tall), tall)
            acc[0, place, :] += product(q, 0, half)
            handed = remote(
                acc.at[0, place], from_partner.at[it, half],
                pair_send.at[it, half], pair_recv.at[it, half], partner,
            )
            begin(handed)
            term = product(q, 1, half)
            handed.wait_recv()
            acc[1, place, :] += term + from_partner[it, half]
            for g in ((3, 2) if half is far else (1, 0)):
                for kind, (col, target) in enumerate(
                    ((both, to_both), (first, to_first), (second, to_second))
                ):
                    begin(scatter(kind, order[g], col, target))

        def reduced(plane):
            which = at(plane, self_)
            value = acc[1, piece(which), :]
            for kind in (1, 2, 0):
                scatter(kind, plane, self_, partner).wait_recv()
                value = value + received[it, kind, which]
            return value

        for g in (3, 2, 1):
            acc[1, piece(at(order[g], self_)), :] = reduced(order[g])
            begin(to_plane(order[g], z))
        summed = reduced(z)
        for g in (1, 2, 3):
            to_plane(order[g], order[g]).wait_recv()
            summed = summed + received[it, 3, order[g]]
        mine = (source[...] - summed) / gap
        if it + 1 < ITERS:
            gathered[it + 1, own] = mine
            later = start_gather(it + 1)
        else:
            out[...] = mine
            later = []
        for copy in sends:
            copy.wait_send()
        sends = later


def fused(sizes, source, vir_energy, occ_energy, factor_vv, factor_oo):
    naux, ngrp = sizes
    rows, width = source.shape
    terms, whole, _ = factor_vv.shape
    chips = naux * ngrp // 2
    span = whole // GROUPS
    tall = chips // HALVES * rows
    vmem = pl.BlockSpec(memory_space=pltpu.VMEM)
    dma = pltpu.SemaphoreType.DMA
    return pl.pallas_call(
        functools.partial(kernel, (naux, ngrp, rows)),
        out_shape=jax.ShapeDtypeStruct((rows, width), F32),
        in_specs=[vmem] * 4 + [pl.BlockSpec(memory_space=pl.ANY)],
        out_specs=vmem,
        scratch_shapes=[
            pltpu.VMEM((2, terms, chips, rows, whole), F32),
            pltpu.VMEM((GROUPS, terms, 2, chips * rows, span), BF16),
            pltpu.VMEM((GROUPS, terms, 2, chips * rows, span), BF16),
            pltpu.VMEM((terms, width, width), BF16),
            pltpu.VMEM((terms, width, width), BF16),
            pltpu.VMEM((terms, span, width), BF16),
            pltpu.VMEM((terms, span, width), BF16),
            pltpu.VMEM((2, chips * rows, width), F32),
            pltpu.VMEM((ITERS, 2 * chips, rows, width), F32),
            pltpu.VMEM((ITERS, HALVES, tall, width), F32),
            pltpu.VMEM((ITERS, 4, chips, rows, width), F32),
            dma((2, terms)),
            dma((ITERS, 5, chips)),
            dma((ITERS, 2 * chips)),
            dma((ITERS, HALVES)),
            dma((ITERS, HALVES)),
            dma((ITERS, 4, chips)),
            dma((ITERS, 4, chips)),
        ],
        compiler_params=pltpu.CompilerParams(collective_id=0, has_side_effects=True),
    )(
        source,
        vir_energy.reshape(1, rows),
        occ_energy.reshape(1, width),
        factor_oo,
        factor_vv.reshape(terms, chips, 2, rows, whole),
    )


def plain(source, vir_energy, occ_energy, factor_vv, factor_oo):
    gap = vir_energy[:, None] - occ_energy[None, :]
    einsum = functools.partial(
        jnp.einsum, precision=lax.Precision.HIGHEST, preferred_element_type=F32
    )
    mine = source / gap
    for _ in range(ITERS):
        whole = lax.all_gather(mine, AXES, axis=0, tiled=True)
        terms = einsum("pab,pbj->aj", factor_vv, einsum("bi,pij->pbj", whole, factor_oo))
        summed = lax.psum_scatter(terms, AXES, scatter_dimension=0, tiled=True)
        mine = (source - summed) / gap
    return mine


def local(sizes, source, *rest):
    chips = sizes[0] * sizes[1] // 2
    rows, width = source.shape
    whole = chips * 2 * rows
    fits = (
        rows % 16 == 0 and sizes == (2 * GROUPS, 4) and GROUPS == 4 and HALVES == 2
        and whole % (GROUPS * 128) == 0 and width % 128 == 0
    )
    return fused(sizes, source, *rest) if fits else plain(source, *rest)


def solution(mesh):
    sizes = (mesh.shape["aux"], mesh.shape["grp"])
    placed = (P(AXES, None), P(AXES), P(), P(AXES, None, None), P(AXES, None, None))
    return jax.shard_map(
        functools.partial(local, sizes),
        mesh=mesh, in_specs=placed, out_specs=P(AXES, None), check_vma=False,
    )
```

```python
import functools

import jax
import jax.numpy as jnp
from jax import lax
from jax.experimental import pallas as pl
from jax.experimental.pallas import tpu as pltpu
from jax.sharding import PartitionSpec as P

ITERS = 2
AXES = ("aux", "grp")
F32 = jnp.float32
BF16 = jnp.bfloat16
MESH = pl.DeviceIdType.MESH
GROUPS = 4
HALVES = 2


def split(value):
    high = value.astype(BF16)
    return high, (value - high.astype(F32)).astype(BF16)


def dot3(a, b):
    (ah, al), (bh, bl) = a, b
    dot = functools.partial(jnp.dot, preferred_element_type=F32)
    return dot(ah, bh) + (dot(ah, bl) + dot(al, bh))


def kernel(
    sizes, source, vir, occ, oo, vv, out,
    stage, vh, vl, oh, ol, th, tl, acc, gathered, from_partner, received,
    load_sem, gather_send, gather_recv, pair_send, pair_recv, scatter_send, scatter_recv,
):
    naux, ngrp, rows = sizes
    chips, pairs = naux * ngrp // 2, ngrp // 2
    terms, width = oo.shape[0], oo.shape[1]
    per_group = chips // GROUPS
    span = 2 * per_group * rows
    per_half = chips // HALVES
    tall = per_half * rows
    aux, grp = lax.axis_index("aux"), lax.axis_index("grp")
    core = grp % 2
    chip = aux * pairs + grp // 2

    def device(which, side):
        return (which // pairs, (which % pairs) * 2 + side)

    z, x, y = aux // 2, aux % 2, grp // 2

    def column(dx, dy):
        return ((x + dx) % 2) * 2 + (y + dy) % 2

    self_, first, second, both = column(0, 0), column(1 - core, core), column(core, 1 - core), column(1, 1)

    def at(plane, col):
        return plane * 4 + col

    partner = device(chip, 1 - core)
    to_first, to_second, to_both = [device(at(z, col), core) for col in (first, second, both)]

    loads = []
    for slot in range(2):
        side = (1 - core) if slot == 0 else core
        for p in range(terms):
            load = pltpu.make_async_copy(vv.at[p, :, side], stage.at[slot, p], load_sem.at[slot, p])
            load.start()
            loads.append(load)

    barrier = pltpu.get_barrier_semaphore()
    pl.semaphore_signal(barrier, inc=1, device_id=partner, device_id_type=MESH)
    order = [z, z + 1 - 2 * (z % 2), 2 - z // 2, 3 - 3 * (z // 2)]
    greeted = [to_first, to_second, to_both] + [device(at(plane, self_), core) for plane in order[1:]]
    for other in greeted:
        pl.semaphore_signal(barrier, inc=1, device_id=other, device_id_type=MESH)

    at_row = lax.broadcasted_iota(jnp.int32, (rows, rows), 0)
    at_column = lax.broadcasted_iota(jnp.int32, (rows, rows), 1)
    spread = jnp.broadcast_to(vir[...], (rows, rows))
    vir_column = jnp.sum(jnp.where(at_row == at_column, spread, 0.0), axis=1, keepdims=True)
    gap = vir_column - occ[...]
    mine = source[...] / gap
    own = 2 * chip + core
    gathered[0, own] = mine
    for p in range(terms):
        oh[p], ol[p] = split(oo[p])
    pl.semaphore_wait(barrier, 1 + len(greeted))

    def remote(src, dst, send, recv, target):
        return pltpu.make_async_remote_copy(
            src, dst, send, recv, device_id=target, device_id_type=MESH
        )

    def block_copy(it, block, kind, index, target):
        piece = gathered.at[it, block]
        return remote(piece, piece, gather_send.at[it, kind, index], gather_recv.at[it, block], target)

    def arrived(it, which, side):
        block_copy(it, 2 * which + side, 0, which, partner).wait_recv()

    def pass_on(it, which, sends, targets):
        for kind, target in targets:
            sends.append(block_copy(it, 2 * which + core, kind, which, target))
            sends[-1].start()

    everyone = ((4, to_both), (0, to_first), (1, to_second), (2, partner))

    def start_gather(it):
        sends = []
        for plane in order[1:]:
            there = at(plane, self_)
            sends.append(block_copy(it, own, 3, there, device(there, core)))
            sends[-1].start()
        pass_on(it, chip, sends, everyone)
        return sends

    def product(q, slot, half):
        place = pl.ds(pl.multiple_of(half * tall, tall), tall)
        total = None
        for p in range(terms):
            term = dot3(
                (vh[q, p, slot, place, :], vl[q, p, slot, place, :]), (th[p], tl[p])
            )
            total = term if total is None else total + term
        return total

    def halfway(it, q):
        piece = gathered[it, pl.ds(q * 2 * per_group, 2 * per_group)].reshape(span, width)
        piece = split(piece)
        for p in range(terms):
            th[p], tl[p] = split(dot3(piece, (oh[p], ol[p])))

    sends = start_gather(0)

    for slot in range(2):
        for p in range(terms):
            loads[slot * terms + p].wait()

            def convert(c, carry):
                value = stage[slot, p, c]
                high, low = split(value)
                place = pl.ds(pl.multiple_of(c * rows, rows), rows)
                for q in range(GROUPS):
                    vh[q, p, slot, place, :] = high[:, q * span:(q + 1) * span]
                    vl[q, p, slot, place, :] = low[:, q * span:(q + 1) * span]
                return carry

            lax.fori_loop(0, chips, convert, 0)

    near = chip // per_half
    far = (near + 1) % HALVES

    for it in range(ITERS):
        def from_plane(g):
            which = at(order[g], self_)
            arrived(it, which, core)
            pass_on(it, which, sends, everyone)

        def from_near(g):
            for col in (first, second, both):
                which = at(order[g], col)
                arrived(it, which, core)
                pass_on(it, which, sends, ((2, partner),))

        def consume(g):
            for col in (self_, first, second, both):
                arrived(it, at(order[g], col), 1 - core)
            halfway(it, order[g])
            return order[g]

        def accumulate(g):
            q = consume(g)

            def step(i, carry):
                slot, half = i // HALVES, i % HALVES
                place = pl.ds(pl.multiple_of(half * tall, tall), tall)
                term = product(q, slot, half)
                if g == 0:
                    acc[slot, place, :] = term
                else:
                    acc[slot, place, :] += term
                return carry

            lax.fori_loop(0, 2 * HALVES, step, 0)

        from_plane(1)
        from_near(0)
        from_plane(2)
        accumulate(0)
        from_plane(3)
        from_near(1)
        from_near(2)
        accumulate(1)
        from_near(3)
        accumulate(2)
        q = consume(3)

        def piece(which):
            return pl.ds(pl.multiple_of(which * rows, rows), rows)

        def scatter(stage_, plane, col, target):
            which = at(plane, col)
            return remote(
                acc.at[1, piece(which)], received.at[it, stage_, which],
                scatter_send.at[it, stage_, which], scatter_recv.at[it, stage_, which], target,
            )

        def to_plane(plane, sender):
            return remote(
                acc.at[1, piece(at(plane, self_))], received.at[it, 3, sender],
                scatter_send.at[it, 3, plane], scatter_recv.at[it, 3, sender],
                device(at(plane, self_), core),
            )

        def begin(copy):
            sends.append(copy)
            copy.start()

        for half in (far, near):
            place = pl.ds(pl.multiple_of(half * tall, tall), tall)
            acc[0, place, :] += product(q, 0, half)
            handed = remote(
                acc.at[0, place], from_partner.at[it, half],
                pair_send.at[it, half], pair_recv.at[it, half], partner,
            )
            begin(handed)
            term = product(q, 1, half)
            handed.wait_recv()
            acc[1, place, :] += term + from_partner[it, half]
            for g in ((3, 2) if half is far else (1, 0)):
                for kind, (col, target) in enumerate(
                    ((both, to_both), (first, to_first), (second, to_second))
                ):
                    begin(scatter(kind, order[g], col, target))

        def reduced(plane):
            which = at(plane, self_)
            value = acc[1, piece(which), :]
            for kind in (1, 2, 0):
                scatter(kind, plane, self_, partner).wait_recv()
                value = value + received[it, kind, which]
            return value

        for g in (3, 2, 1):
            acc[1, piece(at(order[g], self_)), :] = reduced(order[g])
            begin(to_plane(order[g], z))
        summed = reduced(z)
        for g in (1, 2, 3):
            to_plane(order[g], order[g]).wait_recv()
            summed = summed + received[it, 3, order[g]]
        mine = (source[...] - summed) / gap
        if it + 1 < ITERS:
            gathered[it + 1, own] = mine
            later = start_gather(it + 1)
        else:
            out[...] = mine
            later = []
        for copy in sends:
            copy.wait_send()
        sends = later


def fused(sizes, source, vir_energy, occ_energy, factor_vv, factor_oo):
    naux, ngrp = sizes
    rows, width = source.shape
    terms, whole, _ = factor_vv.shape
    chips = naux * ngrp // 2
    span = whole // GROUPS
    tall = chips // HALVES * rows
    vmem = pl.BlockSpec(memory_space=pltpu.VMEM)
    dma = pltpu.SemaphoreType.DMA
    return pl.pallas_call(
        functools.partial(kernel, (naux, ngrp, rows)),
        out_shape=jax.ShapeDtypeStruct((rows, width), F32),
        in_specs=[vmem] * 4 + [pl.BlockSpec(memory_space=pl.ANY)],
        out_specs=vmem,
        scratch_shapes=[
            pltpu.VMEM((2, terms, chips, rows, whole), F32),
            pltpu.VMEM((GROUPS, terms, 2, chips * rows, span), BF16),
            pltpu.VMEM((GROUPS, terms, 2, chips * rows, span), BF16),
            pltpu.VMEM((terms, width, width), BF16),
            pltpu.VMEM((terms, width, width), BF16),
            pltpu.VMEM((terms, span, width), BF16),
            pltpu.VMEM((terms, span, width), BF16),
            pltpu.VMEM((2, chips * rows, width), F32),
            pltpu.VMEM((ITERS, 2 * chips, rows, width), F32),
            pltpu.VMEM((ITERS, HALVES, tall, width), F32),
            pltpu.VMEM((ITERS, 4, chips, rows, width), F32),
            dma((2, terms)),
            dma((ITERS, 5, chips)),
            dma((ITERS, 2 * chips)),
            dma((ITERS, HALVES)),
            dma((ITERS, HALVES)),
            dma((ITERS, 4, chips)),
            dma((ITERS, 4, chips)),
        ],
        compiler_params=pltpu.CompilerParams(collective_id=0, has_side_effects=True),
    )(
        source,
        vir_energy.reshape(1, rows),
        occ_energy.reshape(1, width),
        factor_oo,
        factor_vv.reshape(terms, chips, 2, rows, whole),
    )


def plain(source, vir_energy, occ_energy, factor_vv, factor_oo):
    gap = vir_energy[:, None] - occ_energy[None, :]
    einsum = functools.partial(
        jnp.einsum, precision=lax.Precision.HIGHEST, preferred_element_type=F32
    )
    mine = source / gap
    for _ in range(ITERS):
        whole = lax.all_gather(mine, AXES, axis=0, tiled=True)
        terms = einsum("pab,pbj->aj", factor_vv, einsum("bi,pij->pbj", whole, factor_oo))
        summed = lax.psum_scatter(terms, AXES, scatter_dimension=0, tiled=True)
        mine = (source - summed) / gap
    return mine


def local(sizes, source, *rest):
    chips = sizes[0] * sizes[1] // 2
    rows, width = source.shape
    whole = chips * 2 * rows
    fits = (
        rows % 16 == 0 and sizes == (2 * GROUPS, 4) and GROUPS == 4 and HALVES == 2
        and whole % (GROUPS * 128) == 0 and width % 128 == 0
    )
    return fused(sizes, source, *rest) if fits else plain(source, *rest)


def solution(mesh):
    sizes = (mesh.shape["aux"], mesh.shape["grp"])
    placed = (P(AXES, None), P(AXES), P(), P(AXES, None, None), P(AXES, None, None))
    return jax.shard_map(
        functools.partial(local, sizes),
        mesh=mesh, in_specs=placed, out_specs=P(AXES, None), check_vma=False,
    )
```
